32 devices in a mesh: feat: 4 (over y, core), rows: 8 (over z, x).
Axes of the slice: x: 2, y: 2, z: 4, core: 2. Of those that a mesh axis runs over, the one named last changes fastest.
Arguments:
- bin_index: int32 [64, 65536], P('feat', 'rows'), may hold values from 0 to 255
- node_ids: int32 [65536], P('rows'), may hold values from 0 to 7
- gradients: int32 [65536], P('rows'), may hold values from -32 to 32
- hessians: int32 [65536], P('rows'), may hold values from 1 to 32
Outputs:
- split_gains: float32 [8, 64, 256], P('rows', 'feat')
- best_gains: float32 [8], P('rows')
The draws below stay inside these ranges and needn't reach their ends.
All inputs are finite; a program needn't handle non-finite values.
Results may differ from the reference program's by a relative error of at most 0.0003.
Values sent between devices are 32-bit elements; how exact they have to be, the bound alone decides.
No kernel may reach another device: no remote copies, remote signals or barrier semaphores. Data moves between devices by JAX's collectives and lax.ppermute only.
A program may use at most 64 MiB of HBM per device.

```python
import math
import jax
import jax.numpy as jnp
import numpy as np

BINS = 256
ROWS = 65536
FEATURES = 64
NODES = 8


def with_ends(result, stream_key, least, largest):
    longest = result.shape.index(max(result.shape))
    spots = []
    for shift in (0, 1):
        where = [jax.random.randint(jax.random.fold_in(stream_key, axis), (), 0, length) for axis, length in enumerate(result.shape)]
        where[longest] = (where[longest] + shift) % result.shape[longest]
        spots.append(tuple(where))
    return result.at[spots[0]].set(least).at[spots[1]].set(largest)


def rank_bounds(count, lean):
    weights = [(1 << 20) // math.isqrt(grade ** lean) + 1 for grade in range(1, count + 1)]
    spread = 1 + sum(weights) // (1 << 30)
    return np.cumsum(np.array([max(1, weight // spread) for weight in weights]))


def ranked_ids(own_key, dims, number_of, lean):
    grid = rank_bounds(number_of, lean)
    ticket = jax.random.randint(jax.random.fold_in(own_key, 1), dims, 0, int(grid[number_of - 1]))
    rank = jnp.searchsorted(jnp.asarray(grid, jnp.int32), ticket, side="right")
    return jax.random.permutation(jax.random.fold_in(own_key, 2), number_of)[rank].astype(jnp.int32)


def setup_inputs(seed: int = 0) -> dict:
    seeds = jax.random.split(jax.random.key(seed), 5)
    bin_index = with_ends(jax.random.randint(seeds[0], (FEATURES, ROWS), 0, BINS), jax.random.fold_in(seeds[0], 1), 0, BINS - 1).astype(jnp.int32)
    node_ids = with_ends(ranked_ids(seeds[1], (ROWS,), NODES, 2), jax.random.fold_in(seeds[1], 3), 0, NODES - 1).astype(jnp.int32)
    gradients = with_ends(jax.random.randint(seeds[2], (ROWS,), -32, 33), jax.random.fold_in(seeds[2], 1), -32, 32).astype(jnp.int32)
    hessians = with_ends(jax.random.randint(seeds[3], (ROWS,), 1, 33), jax.random.fold_in(seeds[3], 1), 1, 32).astype(jnp.int32)
    return dict(bin_index=bin_index, node_ids=node_ids, gradients=gradients, hessians=hessians)


shrinkage = 1.0


def gains_of(grad_hist, hess_hist):
    left_grad = jnp.cumsum(grad_hist, axis=-1)
    left_hess = jnp.cumsum(hess_hist, axis=-1)
    total_grad = left_grad[..., -1:]
    total_hess = left_hess[..., -1:]
    right_grad = total_grad - left_grad
    right_hess = total_hess - left_hess
    return 0.5 * (left_grad * left_grad / (left_hess + shrinkage) + right_grad * right_grad / (right_hess + shrinkage) - total_grad * total_grad / (total_hess + shrinkage))


def reference(bin_index, node_ids, gradients, hessians):
    row_major = bin_index.T
    feature_ids = jnp.arange(FEATURES, dtype=jnp.int32)
    segment = ((node_ids[:, None] * FEATURES + feature_ids[None, :]) * BINS + row_major).astype(jnp.int32).reshape(-1)
    grad_rows = jnp.broadcast_to(gradients.astype(jnp.float32)[:, None], row_major.shape).reshape(-1)
    hess_rows = jnp.broadcast_to(hessians.astype(jnp.float32)[:, None], row_major.shape).reshape(-1)
    grad_hist = jax.ops.segment_sum(grad_rows, segment, NODES * FEATURES * BINS).reshape(NODES, FEATURES, BINS)
    hess_hist = jax.ops.segment_sum(hess_rows, segment, NODES * FEATURES * BINS).reshape(NODES, FEATURES, BINS)
    split_gains = gains_of(grad_hist, hess_hist)
    best_gains = jnp.max(split_gains, axis=(1, 2))
    return split_gains, best_gains
```

```python
import functools

import jax
import jax.numpy as jnp
from jax import lax
from jax.experimental import pallas as pl
from jax.experimental.pallas import tpu as pltpu
from jax.sharding import PartitionSpec as P

BINS = 256
LANES = 128
HIGH = 4
LOW = BINS // HIGH
NODE_ROWS = 2 * HIGH

shrinkage = 1.0


def histogram_kernel(bin_ref, node_ref, grad_ref, hess_ref, table_ref, row_key, low_key, weight):
    feature_count, row_count = bin_ref.shape
    node_count, pair_count = table_ref.shape[:2]
    product_rows = node_count * NODE_ROWS

    bins = bin_ref[...]
    row_key[...] = node_ref[...] * HIGH + bins // LOW
    low_key[...] = bins & (LOW - 1)
    slot = lax.broadcasted_iota(jnp.int32, (2 * NODE_ROWS, row_count), 0)
    is_grad = (slot & HIGH) == 0
    value = jnp.where(is_grad, grad_ref[...], hess_ref[...])
    weight[...] = value.astype(jnp.float32).astype(jnp.bfloat16)

    slot = lax.broadcasted_iota(jnp.int32, (product_rows, row_count), 0)
    wanted_row = ((slot // NODE_ROWS) * HIGH + (slot & (HIGH - 1))).astype(jnp.int16)
    wanted_low = lax.broadcasted_iota(jnp.int32, (LOW, row_count), 0).astype(jnp.int16)
    zero = jnp.zeros((), jnp.bfloat16)
    one = jnp.ones((), jnp.bfloat16)
    first_half = lax.broadcasted_iota(jnp.int32, (product_rows, LANES), 1) < LOW

    def one_hots(feature):
        key = jnp.broadcast_to(row_key[pl.ds(feature, 1), :], (product_rows, row_count))
        low = jnp.broadcast_to(low_key[pl.ds(feature, 1), :], (LOW, row_count))
        values = jnp.concatenate([weight[...]] * (product_rows // (2 * NODE_ROWS)), axis=0)
        left = jnp.where(key.astype(jnp.int16) == wanted_row, values, zero)
        right = jnp.where(low.astype(jnp.int16) == wanted_low, one, zero)
        return left, right

    @pl.loop(0, pair_count, unroll=2)
    def _(pair):
        left_a, right_a = one_hots(pair)
        left_b, right_b = one_hots(pair + pair_count)
        both = lax.dot_general(
            jnp.concatenate([left_a, left_b], axis=0),
            jnp.concatenate([right_a, right_b], axis=0),
            (((1,), (1,)), ((), ())),
            preferred_element_type=jnp.float32,
        )
        own = jnp.where(first_half, both[:product_rows], both[product_rows:])
        table_ref[:, pair] = own.reshape(node_count, NODE_ROWS, LANES)


def histograms(bin_index, node_ids, gradients, hessians, node_count):
    feature_count, row_count = bin_index.shape
    return pl.pallas_call(
        histogram_kernel,
        out_shape=jax.ShapeDtypeStruct(
            (node_count, feature_count // 2, NODE_ROWS, LANES), jnp.float32
        ),
        scratch_shapes=[
            pltpu.VMEM((feature_count, row_count), jnp.int32),
            pltpu.VMEM((feature_count, row_count), jnp.int32),
            pltpu.VMEM((2 * NODE_ROWS, row_count), jnp.bfloat16),
        ],
        name="histograms",
    )(
        bin_index,
        node_ids.reshape(1, row_count),
        gradients.reshape(1, row_count),
        hessians.reshape(1, row_count),
    )


def prefix_sums(first, second):
    lane = lax.broadcasted_iota(jnp.int32, first.shape, 1)
    step = 1
    while step < LANES:
        first = first + jnp.where(lane >= step, pltpu.roll(first, step, axis=1), 0.0)
        second = second + jnp.where(lane >= step, pltpu.roll(second, step, axis=1), 0.0)
        step *= 2
    return first, second + first[:, LANES - 1 :]


def gains_kernel(parts_ref, gains_ref, best_ref, table):
    pair_count = parts_ref.shape[1]
    table[...] = jnp.sum(parts_ref[...], axis=0).reshape(pair_count * NODE_ROWS, LANES)
    lane = lax.broadcasted_iota(jnp.int32, (pair_count, LANES), 1)
    sums = []
    for value in range(2):
        rows = [
            table[pl.ds(value * HIGH + high, pair_count, stride=NODE_ROWS), :]
            for high in range(HIGH)
        ]
        turned = [pltpu.roll(row, LOW, axis=1) for row in rows]
        halves = []
        for half in range(2):
            tiles = []
            for at in range(0, HIGH, 2):
                left = rows[at] if half == 0 else turned[at]
                right = turned[at + 1] if half == 0 else rows[at + 1]
                tiles.append(jnp.where(lane < LOW, left, right))
            halves.append(prefix_sums(*tiles))
        sums.append(halves)
    best = None
    for half in range(2):
        grad, hess = sums[0][half], sums[1][half]
        total_grad = grad[1][:, LANES - 1 :]
        total_hess = hess[1][:, LANES - 1 :]
        whole = total_grad * total_grad / (total_hess + shrinkage)
        for at in range(2):
            left_grad, left_hess = grad[at], hess[at]
            right_grad = total_grad - left_grad
            right_hess = total_hess - left_hess
            gains = 0.5 * (
                left_grad * left_grad / (left_hess + shrinkage)
                + right_grad * right_grad / (right_hess + shrinkage)
                - whole
            )
            gains_ref[0, pl.ds(half * pair_count, pair_count), pl.ds(at * LANES, LANES)] = gains
            best = gains if best is None else jnp.maximum(best, gains)
    best_ref[0] = jnp.max(best)


def split_gains_of(parts):
    pair_count = parts.shape[1]
    return pl.pallas_call(
        gains_kernel,
        out_shape=(
            jax.ShapeDtypeStruct((1, 2 * pair_count, BINS), jnp.float32),
            jax.ShapeDtypeStruct((1,), jnp.float32),
        ),
        out_specs=(
            pl.BlockSpec(memory_space=pltpu.VMEM),
            pl.BlockSpec(memory_space=pltpu.SMEM),
        ),
        scratch_shapes=[pltpu.VMEM((pair_count * NODE_ROWS, LANES), jnp.float32)],
        name="gains",
    )(parts)


def per_device(bin_index, node_ids, gradients, hessians):
    node_count = lax.axis_size("rows")
    table = histograms(bin_index, node_ids, gradients, hessians, node_count)
    parts = lax.all_to_all(table, "rows", 0, 0, tiled=True)
    split_gains, local_best = split_gains_of(parts)
    best_gains = lax.pmax(local_best, "feat")
    return split_gains, best_gains


def solution(mesh):
    in_specs = (P("feat", "rows"), P("rows"), P("rows"), P("rows"))
    out_specs = (P("rows", "feat", None), P("rows"))
    return jax.shard_map(
        per_device, mesh=mesh, in_specs=in_specs, out_specs=out_specs, check_vma=False
    )
```

```python
import jax
import jax.numpy as jnp
from jax import lax
from jax.experimental import pallas as pl
from jax.experimental.pallas import tpu as pltpu
from jax.sharding import PartitionSpec as P


BINS = 256
LANES = 128
SUBLANES = 8
HIGH = 4
LOW = BINS // HIGH
NODE_ROWS = 2 * HIGH
PAIRS = SUBLANES // 2

shrinkage = 1.0


def bit_count(length):
    return length.bit_length() - 1


def reversed_bits(number, bits):
    return sum(((number >> bit) & 1) << (bits - 1 - bit) for bit in range(bits))


def histogram_kernel(
    bin_hbm, node_hbm, grad_hbm, hess_hbm, table_ref, bins, small, row_key, low_key, weight, sems
):
    feature_count, row_count = bins.shape
    node_count = table_ref.shape[0]
    bits = bit_count(node_count)
    product_rows = node_count * NODE_ROWS
    groups = feature_count // SUBLANES

    def rows_of(group):
        return pl.ds(group * SUBLANES, SUBLANES)

    small_copies = [
        pltpu.make_async_copy(source, small.at[at], sems.at[at])
        for at, source in enumerate((node_hbm, grad_hbm, hess_hbm))
    ]
    bin_copies = [
        pltpu.make_async_copy(bin_hbm.at[rows_of(group)], bins.at[rows_of(group)], sems.at[3 + group])
        for group in range(groups)
    ]
    for copy in small_copies + bin_copies:
        copy.start()
    for copy in small_copies:
        copy.wait()

    slot = lax.broadcasted_iota(jnp.int32, (2 * NODE_ROWS, row_count), 0)
    value = jnp.where((slot & HIGH) == 0, small[1], small[2])
    weight[...] = value.astype(jnp.float32).astype(jnp.bfloat16)

    slot = lax.broadcasted_iota(jnp.int32, (product_rows, row_count), 0)
    wanted_row = ((slot >> bit_count(NODE_ROWS)) * HIGH + (slot & (HIGH - 1))).astype(jnp.int16)
    wanted_low = lax.broadcasted_iota(jnp.int32, (LOW, row_count), 0).astype(jnp.int16)
    zero = jnp.zeros((), jnp.bfloat16)
    one = jnp.ones((), jnp.bfloat16)
    first_half = lax.broadcasted_iota(jnp.int32, (product_rows, LANES), 1) < LOW
    me = reversed_bits(lax.axis_index("rows"), bits)

    def one_hots(feature):
        key = jnp.broadcast_to(row_key[pl.ds(feature, 1), :], (product_rows, row_count))
        low = jnp.broadcast_to(low_key[pl.ds(feature, 1), :], (LOW, row_count))
        values = jnp.concatenate([weight[...]] * (product_rows // (2 * NODE_ROWS)), axis=0)
        left = jnp.where(key.astype(jnp.int16) == wanted_row, values, zero)
        right = jnp.where(low.astype(jnp.int16) == wanted_low, one, zero)
        return left, right

    @pl.loop(0, groups)
    def _(group):
        pltpu.make_async_copy(
            bin_hbm.at[rows_of(0)], bins.at[rows_of(0)], sems.at[3 + group]
        ).wait()
        here = bins[pl.ds(pl.multiple_of(group * SUBLANES, SUBLANES), SUBLANES), :]
        row_key[...] = small[0] * HIGH + (here >> bit_count(LOW))
        low_key[...] = here & (LOW - 1)
        for pair in range(PAIRS):
            left_a, right_a = one_hots(pair)
            left_b, right_b = one_hots(pair + PAIRS)
            both = lax.dot_general(
                jnp.concatenate([left_a, left_b], axis=0),
                jnp.concatenate([right_a, right_b], axis=0),
                (((1,), (1,)), ((), ())),
                preferred_element_type=jnp.float32,
            )
            own = jnp.where(first_half, both[:product_rows], both[product_rows:])
            for node in range(node_count):
                table_ref[reversed_bits(node, bits) ^ me, group * PAIRS + pair] = own[
                    node * NODE_ROWS : (node + 1) * NODE_ROWS
                ]


def histograms(bin_index, node_ids, gradients, hessians, node_count):
    feature_count, row_count = bin_index.shape
    return pl.pallas_call(
        histogram_kernel,
        out_shape=jax.ShapeDtypeStruct(
            (node_count, feature_count // 2, NODE_ROWS, LANES), jnp.float32
        ),
        in_specs=[pl.BlockSpec(memory_space=pltpu.HBM)] * 4,
        out_specs=pl.BlockSpec(memory_space=pltpu.VMEM),
        scratch_shapes=[
            pltpu.VMEM((feature_count, row_count), jnp.int32),
            pltpu.VMEM((3, 1, row_count), jnp.int32),
            pltpu.VMEM((SUBLANES, row_count), jnp.int32),
            pltpu.VMEM((SUBLANES, row_count), jnp.int32),
            pltpu.VMEM((2 * NODE_ROWS, row_count), jnp.bfloat16),
            pltpu.SemaphoreType.DMA((3 + feature_count // SUBLANES,)),
        ],
        compiler_params=pltpu.CompilerParams(vmem_limit_bytes=16 << 20),
        name="histograms",
    )(
        *(
            pltpu.with_memory_space_constraint(array, pltpu.HBM)
            for array in (
                bin_index,
                node_ids.reshape(1, row_count),
                gradients.reshape(1, row_count),
                hessians.reshape(1, row_count),
            )
        )
    )


def prefix_sums(first, second):
    lane = lax.broadcasted_iota(jnp.int32, first.shape, 1)
    step = 1
    while step < LANES:
        first = first + jnp.where(lane >= step, pltpu.roll(first, step, axis=1), 0.0)
        second = second + jnp.where(lane >= step, pltpu.roll(second, step, axis=1), 0.0)
        step *= 2
    return first, second + first[:, LANES - 1 :]


def gains_kernel(*refs):
    parts, (gains_ref, best_ref, table) = refs[:-3], refs[-3:]
    pair_count = parts[0].shape[1]
    whole_table = sum(jnp.sum(part[...], axis=0) for part in parts)
    table[...] = whole_table.reshape(pair_count * NODE_ROWS, LANES)
    lane = lax.broadcasted_iota(jnp.int32, (pair_count, LANES), 1)
    sums = []
    for value in range(2):
        rows = [
            table[pl.ds(value * HIGH + high, pair_count, stride=NODE_ROWS), :]
            for high in range(HIGH)
        ]
        turned = [pltpu.roll(row, LOW, axis=1) for row in rows]
        halves = []
        for half in range(2):
            tiles = []
            for at in range(0, HIGH, 2):
                left = rows[at] if half == 0 else turned[at]
                right = turned[at + 1] if half == 0 else rows[at + 1]
                tiles.append(jnp.where(lane < LOW, left, right))
            halves.append(prefix_sums(*tiles))
        sums.append(halves)
    best = None
    for half in range(2):
        grad, hess = sums[0][half], sums[1][half]
        total_grad = grad[1][:, LANES - 1 :]
        total_hess = hess[1][:, LANES - 1 :]
        whole = total_grad * total_grad / (total_hess + shrinkage)
        for at in range(2):
            left_grad, left_hess = grad[at], hess[at]
            right_grad = total_grad - left_grad
            right_hess = total_hess - left_hess
            gains = 0.5 * (
                left_grad * left_grad / (left_hess + shrinkage)
                + right_grad * right_grad / (right_hess + shrinkage)
                - whole
            )
            for group in range(pair_count // PAIRS):
                gains_ref[
                    0,
                    pl.ds(group * SUBLANES + half * PAIRS, PAIRS),
                    pl.ds(at * LANES, LANES),
                ] = gains[group * PAIRS : (group + 1) * PAIRS]
            best = gains if best is None else jnp.maximum(best, gains)
    best_ref[...] = jnp.full(best_ref.shape, jnp.max(best), jnp.float32)


def split_gains_of(*parts):
    pair_count = parts[0].shape[1]
    return pl.pallas_call(
        gains_kernel,
        out_shape=(
            jax.ShapeDtypeStruct((1, 2 * pair_count, BINS), jnp.float32),
            jax.ShapeDtypeStruct((1, LANES), jnp.float32),
        ),
        in_specs=[pl.BlockSpec(memory_space=pltpu.VMEM)] * len(parts),
        out_specs=[pl.BlockSpec(memory_space=pltpu.VMEM)] * 2,
        scratch_shapes=[pltpu.VMEM((pair_count * NODE_ROWS, LANES), jnp.float32)],
        compiler_params=pltpu.CompilerParams(vmem_limit_bytes=8 << 20),
        name="gains",
    )(*parts)


def swap(array, axis, mask):
    return lax.ppermute(array, axis, [(at, at ^ mask) for at in range(lax.axis_size(axis))])


def reduced(table, phases):
    bit = 0
    kept, received = table, []
    for width in phases:
        for block in received:
            kept = kept + block
        radix = 1 << width
        parts = kept.reshape(radix, kept.shape[0] // radix, *kept.shape[1:])
        received = [
            swap(parts[part], "rows", reversed_bits(part, width) << bit)
            for part in range(1, radix)
        ]
        kept = parts[0]
        bit += width
    return [kept, *received]


def per_device(bin_index, node_ids, gradients, hessians):
    node_count = lax.axis_size("rows")
    table = histograms(bin_index, node_ids, gradients, hessians, node_count)
    phases = [2] + [1] * (bit_count(node_count) - 2)
    split_gains, best = split_gains_of(*reduced(table, phases))
    for bit in range(bit_count(lax.axis_size("feat"))):
        best = jnp.maximum(best, swap(best, "feat", 1 << bit))
    return split_gains, best[0, :1]


def solution(mesh):
    in_specs = (P("feat", "rows"), P("rows"), P("rows"), P("rows"))
    out_specs = (P("rows", "feat", None), P("rows"))
    return jax.shard_map(
        per_device, mesh=mesh, in_specs=in_specs, out_specs=out_specs, check_vma=False
    )
```

```python
import jax
import jax.numpy as jnp
from jax import lax
from jax.experimental import pallas as pl
from jax.experimental.pallas import tpu as pltpu
from jax.sharding import PartitionSpec as P


BINS = 256
LANES = 128
SUBLANES = 8
PACKED = 32
HIGH = 4
LOW = BINS // HIGH
NODE_ROWS = 2 * HIGH
PAIRS = SUBLANES // 2

shrinkage = 1.0


def bit_count(length):
    return length.bit_length() - 1


def phases_of(bits):
    return [[1, 0]] + [[bit] for bit in range(2, bits)]


def place_of(number, bits):
    order = [bit for phase in phases_of(bits) for bit in phase]
    return sum(((number >> bit) & 1) << (bits - 1 - at) for at, bit in enumerate(order))


def histogram_kernel(
    bin_hbm, node_hbm, grad_hbm, hess_hbm, table_ref, bins, small, row_key, low_key, weights, sems
):
    feature_count, row_count = bins.shape
    node_count = table_ref.shape[0]
    bits = bit_count(node_count)
    key_count = node_count * HIGH
    groups = feature_count // SUBLANES

    def rows_of(group):
        return pl.ds(group * SUBLANES, SUBLANES)

    small_copies = [
        pltpu.make_async_copy(source, small.at[at], sems.at[at])
        for at, source in enumerate((node_hbm, grad_hbm, hess_hbm))
    ]
    bin_copies = [
        pltpu.make_async_copy(bin_hbm.at[rows_of(group)], bins.at[rows_of(group)], sems.at[3 + group])
        for group in range(groups)
    ]
    for copy in small_copies + bin_copies:
        copy.start()
    for copy in small_copies:
        copy.wait()

    grad, hess = small[1], small[2]
    shared = (grad & 3) + jnp.where(hess > 16, 8, 0)
    for at, part in enumerate((grad - shared, hess - 2 * shared, shared)):
        part = jnp.broadcast_to(part.astype(jnp.float32), weights.shape[1:])
        weights[at] = part.astype(weights.dtype)

    wanted_key = lax.broadcasted_iota(jnp.int32, (key_count, row_count), 0).astype(jnp.int8)
    wanted_low = lax.broadcasted_iota(jnp.int32, (LOW, row_count), 0).astype(jnp.int8)
    zero = jnp.zeros((), weights.dtype)
    one = jnp.ones((), weights.dtype)
    first_half = lax.broadcasted_iota(jnp.int32, (3 * key_count, LANES), 1) < LOW
    upper = lax.broadcasted_iota(jnp.int32, (SUBLANES, LANES), 0) < HIGH
    me = place_of(lax.axis_index("rows"), bits)

    def one_hots(feature):
        key = jnp.broadcast_to(row_key[pl.ds(feature, 1), :], (key_count, row_count))
        low = jnp.broadcast_to(low_key[pl.ds(feature, 1), :], (LOW, row_count))
        here = key.astype(jnp.int8) == wanted_key
        left = [
            jnp.where(here, jnp.concatenate([weights[at]] * (key_count // PACKED), axis=0), zero)
            for at in range(3)
        ]
        right = jnp.where(low.astype(jnp.int8) == wanted_low, one, zero)
        return left, right

    @pl.loop(0, groups)
    def _(group):
        pltpu.make_async_copy(
            bin_hbm.at[rows_of(0)], bins.at[rows_of(0)], sems.at[3 + group]
        ).wait()
        here = bins[pl.ds(pl.multiple_of(group * SUBLANES, SUBLANES), SUBLANES), :]
        row_key[...] = small[0] * HIGH + (here >> bit_count(LOW))
        low_key[...] = here & (LOW - 1)
        for pair in range(PAIRS):
            left_a, right_a = one_hots(pair)
            left_b, right_b = one_hots(pair + PAIRS)
            both = lax.dot_general(
                jnp.concatenate(left_a + left_b, axis=0),
                jnp.concatenate([right_a, right_b], axis=0),
                (((1,), (1,)), ((), ())),
                preferred_element_type=jnp.float32,
            )
            own = jnp.where(first_half, both[: 3 * key_count], both[3 * key_count :])
            shared_sum = own[2 * key_count :]
            grad_sum = own[:key_count] + shared_sum
            hess_sum = own[key_count : 2 * key_count] + 2.0 * shared_sum
            for first in range(0, node_count, 2):
                two = slice(first * HIGH, first * HIGH + SUBLANES)
                grads, hesses = grad_sum[two], hess_sum[two]
                tiles = (
                    jnp.where(upper, grads, pltpu.roll(hesses, HIGH, axis=0)),
                    jnp.where(upper, pltpu.roll(grads, HIGH, axis=0), hesses),
                )
                for node, tile in zip((first, first + 1), tiles):
                    table_ref[place_of(node, bits) ^ me, group * PAIRS + pair] = tile


def histograms(bin_index, node_ids, gradients, hessians, node_count):
    feature_count, row_count = bin_index.shape
    return pl.pallas_call(
        histogram_kernel,
        out_shape=jax.ShapeDtypeStruct(
            (node_count, feature_count // 2, NODE_ROWS, LANES), jnp.float32
        ),
        in_specs=[pl.BlockSpec(memory_space=pltpu.HBM)] * 4,
        out_specs=pl.BlockSpec(memory_space=pltpu.VMEM),
        scratch_shapes=[
            pltpu.VMEM((feature_count, row_count), jnp.int32),
            pltpu.VMEM((3, 1, row_count), jnp.int32),
            pltpu.VMEM((SUBLANES, row_count), jnp.int32),
            pltpu.VMEM((SUBLANES, row_count), jnp.int32),
            pltpu.VMEM((3, PACKED, row_count), jnp.float8_e4m3fn),
            pltpu.SemaphoreType.DMA((3 + feature_count // SUBLANES,)),
        ],
        compiler_params=pltpu.CompilerParams(vmem_limit_bytes=16 << 20),
        name="histograms",
    )(
        *(
            pltpu.with_memory_space_constraint(array, pltpu.HBM)
            for array in (
                bin_index,
                node_ids.reshape(1, row_count),
                gradients.reshape(1, row_count),
                hessians.reshape(1, row_count),
            )
        )
    )


def summed_over_bins(tiles):
    values = jnp.concatenate(tiles, axis=0)
    parts = []
    for _ in range(3):
        parts.append(values.astype(jnp.bfloat16))
        values = values - parts[-1].astype(jnp.float32)
    source = lax.broadcasted_iota(jnp.int32, (LANES, 2 * LANES), 0)
    column = lax.broadcasted_iota(jnp.int32, (LANES, 2 * LANES), 1)
    counted = jnp.where(source <= column, 1.0, 0.0).astype(jnp.bfloat16)
    sums = lax.dot_general(
        jnp.concatenate(parts, axis=0),
        counted,
        (((1,), (0,)), ((), ())),
        preferred_element_type=jnp.float32,
    )
    count = len(tiles) * tiles[0].shape[0]
    sums = sums[:count] + sums[count : 2 * count] + sums[2 * count :]
    height = tiles[0].shape[0]
    return [
        (sums[at : at + height, :LANES], sums[at : at + height, LANES:])
        for at in range(0, count, height)
    ]


def gains_kernel(*refs):
    parts, (gains_ref, best_ref, table) = refs[:-3], refs[-3:]
    pair_count = parts[0].shape[1]
    whole_table = sum(jnp.sum(part[...], axis=0) for part in parts)
    table[...] = whole_table.reshape(pair_count * NODE_ROWS, LANES)
    lane = lax.broadcasted_iota(jnp.int32, (pair_count, LANES), 1)
    tiles = []
    for value in range(2):
        rows = [
            table[pl.ds(value * HIGH + high, pair_count, stride=NODE_ROWS), :]
            for high in range(HIGH)
        ]
        turned = [pltpu.roll(row, LOW, axis=1) for row in rows]
        for at in range(0, HIGH, 2):
            tiles.append(jnp.where(lane < LOW, rows[at], turned[at + 1]))
        for at in range(0, HIGH, 2):
            tiles.append(jnp.where(lane < LOW, turned[at], rows[at + 1]))
    sums = summed_over_bins(tiles)
    best = None
    for half in range(2):
        (grad_0, total_grad_0), (grad_1, total_grad_1) = sums[2 * half : 2 * half + 2]
        (hess_0, total_hess_0), (hess_1, total_hess_1) = sums[4 + 2 * half : 6 + 2 * half]
        total_grad, total_hess = total_grad_0 + total_grad_1, total_hess_0 + total_hess_1
        whole = total_grad * total_grad / (total_hess + shrinkage)
        lefts = ((grad_0, hess_0), (total_grad_0 + grad_1, total_hess_0 + hess_1))
        for at, (left_grad, left_hess) in enumerate(lefts):
            right_grad = total_grad - left_grad
            right_hess = total_hess - left_hess
            gains = 0.5 * (
                left_grad * left_grad / (left_hess + shrinkage)
                + right_grad * right_grad / (right_hess + shrinkage)
                - whole
            )
            for group in range(pair_count // PAIRS):
                gains_ref[
                    0,
                    pl.ds(group * SUBLANES + half * PAIRS, PAIRS),
                    pl.ds(at * LANES, LANES),
                ] = gains[group * PAIRS : (group + 1) * PAIRS]
            best = gains if best is None else jnp.maximum(best, gains)
    best_ref[...] = best


def split_gains_of(*parts):
    pair_count = parts[0].shape[1]
    return pl.pallas_call(
        gains_kernel,
        out_shape=(
            jax.ShapeDtypeStruct((1, 2 * pair_count, BINS), jnp.float32),
            jax.ShapeDtypeStruct((pair_count, LANES), jnp.float32),
        ),
        in_specs=[pl.BlockSpec(memory_space=pltpu.VMEM)] * len(parts),
        out_specs=[pl.BlockSpec(memory_space=pltpu.VMEM)] * 2,
        scratch_shapes=[pltpu.VMEM((pair_count * NODE_ROWS, LANES), jnp.float32)],
        compiler_params=pltpu.CompilerParams(vmem_limit_bytes=8 << 20),
        name="gains",
    )(*parts)


def outputs_kernel(gains_ref, own_ref, other_ref, gains_out, best_out):
    gains_out[...] = gains_ref[...]
    best_out[0] = jnp.max(jnp.maximum(own_ref[...], other_ref[...]))


def outputs_of(gains, own, other):
    return pl.pallas_call(
        outputs_kernel,
        out_shape=(
            jax.ShapeDtypeStruct(gains.shape, jnp.float32),
            jax.ShapeDtypeStruct((1,), jnp.float32),
        ),
        in_specs=[pl.BlockSpec(memory_space=pltpu.VMEM)] * 3,
        out_specs=(
            pl.BlockSpec(memory_space=pltpu.VMEM),
            pl.BlockSpec(memory_space=pltpu.SMEM),
        ),
        compiler_params=pltpu.CompilerParams(vmem_limit_bytes=2 << 20),
        name="outputs",
    )(gains, own, other)


def swap(array, axis, mask):
    return lax.ppermute(array, axis, [(at, at ^ mask) for at in range(lax.axis_size(axis))])


def reduced(table, phases):
    kept, received = table, []
    for phase in phases:
        for block in received:
            kept = kept + block
        radix = 1 << len(phase)
        parts = kept.reshape(radix, kept.shape[0] // radix, *kept.shape[1:])
        received = []
        for part in range(1, radix):
            mask = sum(((part >> (len(phase) - 1 - at)) & 1) << bit for at, bit in enumerate(phase))
            received.append(swap(parts[part], "rows", mask))
        kept = parts[0]
    return [kept, *received]


def per_device(bin_index, node_ids, gradients, hessians):
    node_count = lax.axis_size("rows")
    table = histograms(bin_index, node_ids, gradients, hessians, node_count)
    split_gains, best = split_gains_of(*reduced(table, phases_of(bit_count(node_count))))
    other = best
    for bit in range(bit_count(lax.axis_size("feat"))):
        best = jnp.maximum(best, other)
        other = swap(best, "feat", (1 << bit) | 1)
    return outputs_of(split_gains, best, other)


def solution(mesh):
    in_specs = (P("feat", "rows"), P("rows"), P("rows"), P("rows"))
    out_specs = (P("rows", "feat", None), P("rows"))
    return jax.shard_map(
        per_device, mesh=mesh, in_specs=in_specs, out_specs=out_specs, check_vma=False
    )
```

```python
import functools

import jax
import jax.numpy as jnp
from jax import lax
from jax.experimental import pallas as pl
from jax.experimental.pallas import tpu as pltpu
from jax.sharding import PartitionSpec as P


BINS = 256
LANES = 128
SUBLANES = 8
PACKED = 32
HIGH = 4
LOW = BINS // HIGH
NODE_ROWS = 2 * HIGH
PAIRS = SUBLANES // 2

shrinkage = 1.0


def bit_count(length):
    return length.bit_length() - 1


def phases_of(bits):
    return [[1, 0]] + [[bit] for bit in range(2, bits)]


def place_of(number, bits):
    order = [bit for phase in phases_of(bits) for bit in phase]
    return sum(((number >> bit) & 1) << (bits - 1 - at) for at, bit in enumerate(order))


def histogram_kernel(
    bin_hbm, node_hbm, grad_hbm, hess_hbm, table_ref, bins, small, row_key, low_key, weights, sems
):
    feature_count, row_count = bins.shape
    node_count = table_ref.shape[0]
    bits = bit_count(node_count)
    key_count = node_count * HIGH
    groups = feature_count // SUBLANES

    def rows_of(group):
        return pl.ds(group * SUBLANES, SUBLANES)

    small_copies = [
        pltpu.make_async_copy(source, small.at[at], sems.at[at])
        for at, source in enumerate((node_hbm, grad_hbm, hess_hbm))
    ]
    bin_copies = [
        pltpu.make_async_copy(bin_hbm.at[rows_of(group)], bins.at[rows_of(group)], sems.at[3 + group])
        for group in range(groups)
    ]
    for copy in small_copies + bin_copies:
        copy.start()
    for copy in small_copies:
        copy.wait()

    grad, hess = small[1], small[2]
    shared = (grad & 3) + jnp.where(hess > 16, 8, 0)
    for at, part in enumerate((grad - shared, hess - 2 * shared, shared)):
        part = jnp.broadcast_to(part.astype(jnp.float32), weights.shape[1:])
        weights[at] = part.astype(weights.dtype)

    wanted_key = lax.broadcasted_iota(jnp.int32, (key_count, row_count), 0).astype(jnp.int8)
    wanted_low = lax.broadcasted_iota(jnp.int32, (LOW, row_count), 0).astype(jnp.int8)
    zero = jnp.zeros((), weights.dtype)
    one = jnp.ones((), weights.dtype)
    first_half = lax.broadcasted_iota(jnp.int32, (3 * key_count, LANES), 1) < LOW
    upper = lax.broadcasted_iota(jnp.int32, (SUBLANES, LANES), 0) < HIGH
    me = place_of(lax.axis_index("rows"), bits)

    def one_hots(feature):
        key = jnp.broadcast_to(row_key[pl.ds(feature, 1), :], (key_count, row_count))
        low = jnp.broadcast_to(low_key[pl.ds(feature, 1), :], (LOW, row_count))
        here = key.astype(jnp.int8) == wanted_key
        left = [
            jnp.where(here, jnp.concatenate([weights[at]] * (key_count // PACKED), axis=0), zero)
            for at in range(3)
        ]
        right = jnp.where(low.astype(jnp.int8) == wanted_low, one, zero)
        return left, right

    @pl.loop(0, groups)
    def _(group):
        pltpu.make_async_copy(
            bin_hbm.at[rows_of(0)], bins.at[rows_of(0)], sems.at[3 + group]
        ).wait()
        here = bins[pl.ds(pl.multiple_of(group * SUBLANES, SUBLANES), SUBLANES), :]
        row_key[...] = small[0] * HIGH + (here >> bit_count(LOW))
        low_key[...] = here & (LOW - 1)
        for pair in range(PAIRS):
            left_a, right_a = one_hots(pair)
            left_b, right_b = one_hots(pair + PAIRS)
            both = lax.dot_general(
                jnp.concatenate(left_a + left_b, axis=0),
                jnp.concatenate([right_a, right_b], axis=0),
                (((1,), (1,)), ((), ())),
                preferred_element_type=jnp.float32,
            )
            own = jnp.where(first_half, both[: 3 * key_count], both[3 * key_count :])
            shared_sum = own[2 * key_count :]
            grad_sum = own[:key_count] + shared_sum
            hess_sum = own[key_count : 2 * key_count] + 2.0 * shared_sum
            for first in range(0, node_count, 2):
                two = slice(first * HIGH, first * HIGH + SUBLANES)
                grads, hesses = grad_sum[two], hess_sum[two]
                tiles = (
                    jnp.where(upper, grads, pltpu.roll(hesses, HIGH, axis=0)),
                    jnp.where(upper, pltpu.roll(grads, HIGH, axis=0), hesses),
                )
                for node, tile in zip((first, first + 1), tiles):
                    table_ref[place_of(node, bits) ^ me, group * PAIRS + pair] = tile


def histograms(bin_index, node_ids, gradients, hessians, node_count):
    feature_count, row_count = bin_index.shape
    return pl.pallas_call(
        histogram_kernel,
        out_shape=jax.ShapeDtypeStruct(
            (node_count, feature_count // 2, NODE_ROWS, LANES), jnp.float32
        ),
        in_specs=[pl.BlockSpec(memory_space=pltpu.HBM)] * 4,
        out_specs=pl.BlockSpec(memory_space=pltpu.VMEM),
        scratch_shapes=[
            pltpu.VMEM((feature_count, row_count), jnp.int32),
            pltpu.VMEM((3, 1, row_count), jnp.int32),
            pltpu.VMEM((SUBLANES, row_count), jnp.int32),
            pltpu.VMEM((SUBLANES, row_count), jnp.int32),
            pltpu.VMEM((3, PACKED, row_count), jnp.float8_e4m3fn),
            pltpu.SemaphoreType.DMA((3 + feature_count // SUBLANES,)),
        ],
        compiler_params=pltpu.CompilerParams(vmem_limit_bytes=16 << 20),
        name="histograms",
    )(
        *(
            pltpu.with_memory_space_constraint(array, pltpu.HBM)
            for array in (
                bin_index,
                node_ids.reshape(1, row_count),
                gradients.reshape(1, row_count),
                hessians.reshape(1, row_count),
            )
        )
    )


def summed_over_bins(tiles):
    values = jnp.concatenate(tiles, axis=0)
    parts = []
    for _ in range(3):
        parts.append(values.astype(jnp.bfloat16))
        values = values - parts[-1].astype(jnp.float32)
    source = lax.broadcasted_iota(jnp.int32, (LANES, 2 * LANES), 0)
    column = lax.broadcasted_iota(jnp.int32, (LANES, 2 * LANES), 1)
    counted = jnp.where(source <= column, 1.0, 0.0).astype(jnp.bfloat16)
    sums = lax.dot_general(
        jnp.concatenate(parts, axis=0),
        counted,
        (((1,), (0,)), ((), ())),
        preferred_element_type=jnp.float32,
    )
    count = len(tiles) * tiles[0].shape[0]
    sums = sums[:count] + sums[count : 2 * count] + sums[2 * count :]
    height = tiles[0].shape[0]
    return [
        (sums[at : at + height, :LANES], sums[at : at + height, LANES:])
        for at in range(0, count, height)
    ]


def gains_kernel(own_count, *refs):
    parts, (gains_ref, best_ref, table) = refs[:-3], refs[-3:]
    best = gains_of(parts[:own_count], gains_ref, table)
    if parts[own_count:]:
        best = jnp.maximum(best, gains_of(parts[own_count:], None, table))
    best_ref[...] = best


def gains_of(parts, gains_ref, table):
    pair_count = parts[0].shape[1]
    whole_table = sum(jnp.sum(part[...], axis=0) for part in parts)
    table[...] = whole_table.reshape(pair_count * NODE_ROWS, LANES)
    lane = lax.broadcasted_iota(jnp.int32, (pair_count, LANES), 1)
    tiles = []
    for value in range(2):
        rows = [
            table[pl.ds(value * HIGH + high, pair_count, stride=NODE_ROWS), :]
            for high in range(HIGH)
        ]
        turned = [pltpu.roll(row, LOW, axis=1) for row in rows]
        for at in range(0, HIGH, 2):
            tiles.append(jnp.where(lane < LOW, rows[at], turned[at + 1]))
        for at in range(0, HIGH, 2):
            tiles.append(jnp.where(lane < LOW, turned[at], rows[at + 1]))
    sums = summed_over_bins(tiles)
    best = None
    for half in range(2):
        (grad_0, total_grad_0), (grad_1, total_grad_1) = sums[2 * half : 2 * half + 2]
        (hess_0, total_hess_0), (hess_1, total_hess_1) = sums[4 + 2 * half : 6 + 2 * half]
        total_grad, total_hess = total_grad_0 + total_grad_1, total_hess_0 + total_hess_1
        whole = total_grad * total_grad / (total_hess + shrinkage)
        lefts = ((grad_0, hess_0), (total_grad_0 + grad_1, total_hess_0 + hess_1))
        for at, (left_grad, left_hess) in enumerate(lefts):
            right_grad = total_grad - left_grad
            right_hess = total_hess - left_hess
            gains = 0.5 * (
                left_grad * left_grad / (left_hess + shrinkage)
                + right_grad * right_grad / (right_hess + shrinkage)
                - whole
            )
            if gains_ref is not None:
                for group in range(pair_count // PAIRS):
                    gains_ref[
                        0,
                        pl.ds(group * SUBLANES + half * PAIRS, PAIRS),
                        pl.ds(at * LANES, LANES),
                    ] = gains[group * PAIRS : (group + 1) * PAIRS]
            best = gains if best is None else jnp.maximum(best, gains)
    return best


def split_gains_of(own, others):
    parts = [*own, *others]
    pair_count = parts[0].shape[1]
    return pl.pallas_call(
        functools.partial(gains_kernel, len(own)),
        out_shape=(
            jax.ShapeDtypeStruct((1, 2 * pair_count, BINS), jnp.float32),
            jax.ShapeDtypeStruct((pair_count, LANES), jnp.float32),
        ),
        in_specs=[pl.BlockSpec(memory_space=pltpu.VMEM)] * len(parts),
        out_specs=[pl.BlockSpec(memory_space=pltpu.VMEM)] * 2,
        scratch_shapes=[pltpu.VMEM((pair_count * NODE_ROWS, LANES), jnp.float32)],
        compiler_params=pltpu.CompilerParams(vmem_limit_bytes=8 << 20),
        name="gains",
    )(*parts)


def outputs_kernel(gains_ref, own_ref, other_ref, gains_out, best_out):
    gains_out[...] = gains_ref[...]
    best_out[0] = jnp.max(jnp.maximum(own_ref[...], other_ref[...]))


def outputs_of(gains, own, other):
    return pl.pallas_call(
        outputs_kernel,
        out_shape=(
            jax.ShapeDtypeStruct(gains.shape, jnp.float32),
            jax.ShapeDtypeStruct((1,), jnp.float32),
        ),
        in_specs=[pl.BlockSpec(memory_space=pltpu.VMEM)] * 3,
        out_specs=(
            pl.BlockSpec(memory_space=pltpu.VMEM),
            pl.BlockSpec(memory_space=pltpu.SMEM),
        ),
        compiler_params=pltpu.CompilerParams(vmem_limit_bytes=2 << 20),
        name="outputs",
    )(gains, own, other)


def swap(array, feat_mask, rows_mask):
    feats, nodes = lax.axis_size("feat"), lax.axis_size("rows")
    pairs = [
        (feat * nodes + node, (feat ^ feat_mask) * nodes + (node ^ rows_mask))
        for feat in range(feats)
        for node in range(nodes)
    ]
    return lax.ppermute(array, ("feat", "rows"), pairs)


def halved(table, phases):
    for phase in phases:
        radix = 1 << len(phase)
        parts = table.reshape(radix, table.shape[0] // radix, *table.shape[1:])
        table = parts[0]
        for part in range(1, radix):
            mask = sum(((part >> (len(phase) - 1 - at)) & 1) << bit for at, bit in enumerate(phase))
            table = table + swap(parts[part], 0, mask)
    return table


def per_device(bin_index, node_ids, gradients, hessians):
    node_count = lax.axis_size("rows")
    table = histograms(bin_index, node_ids, gradients, hessians, node_count)
    phases = phases_of(bit_count(node_count))
    *phases, (last,) = phases
    table = halved(table, phases)
    kept, sent = table[:1], table[1:]
    rows_mask = 1 << last
    own = [kept, swap(sent, 0, rows_mask)]
    others, masks = [], [1 << bit for bit in range(bit_count(lax.axis_size("feat")))]
    if len(masks) > 1:
        pair_mask = masks[0] | masks[1]
        others = [swap(kept, pair_mask, 0), swap(sent, pair_mask, rows_mask)]
        masks = [mask | 1 for mask in masks[2:]] + masks[:1]
    split_gains, best = split_gains_of(own, others)
    other = best
    for mask in masks:
        best = jnp.maximum(best, other)
        other = swap(best, mask, 0)
    return outputs_of(split_gains, best, other)


def solution(mesh):
    in_specs = (P("feat", "rows"), P("rows"), P("rows"), P("rows"))
    out_specs = (P("rows", "feat", None), P("rows"))
    return jax.shard_map(
        per_device, mesh=mesh, in_specs=in_specs, out_specs=out_specs, check_vma=False
    )
```

```python
import functools

import jax
import jax.numpy as jnp
from jax import lax
from jax.experimental import pallas as pl
from jax.experimental.pallas import tpu as pltpu
from jax.sharding import PartitionSpec as P


BINS = 256
LANES = 128
SUBLANES = 8
PACKED = 32
HIGH = 4
LOW = BINS // HIGH
NODE_ROWS = 2 * HIGH
PAIRS = SUBLANES // 2

shrinkage = 1.0


def bit_count(length):
    return length.bit_length() - 1


def phases_of(bits):
    return [[1, 0]] + [[bit] for bit in range(2, bits)]


def place_of(number, bits):
    order = [bit for phase in phases_of(bits) for bit in phase]
    return sum(((number >> bit) & 1) << (bits - 1 - at) for at, bit in enumerate(order))


def histogram_kernel(
    bin_hbm, node_hbm, grad_hbm, hess_hbm, table_ref, bins, small, row_key, low_key, weights, sems
):
    feature_count, row_count = bins.shape
    node_count = table_ref.shape[0]
    bits = bit_count(node_count)
    key_count = node_count * HIGH
    groups = feature_count // SUBLANES

    def rows_of(group):
        return pl.ds(group * SUBLANES, SUBLANES)

    small_copies = [
        pltpu.make_async_copy(source, small.at[at], sems.at[at])
        for at, source in enumerate((node_hbm, grad_hbm, hess_hbm))
    ]
    bin_copies = [
        pltpu.make_async_copy(bin_hbm.at[rows_of(group)], bins.at[rows_of(group)], sems.at[3 + group])
        for group in range(groups)
    ]
    for copy in small_copies + bin_copies:
        copy.start()
    for copy in small_copies:
        copy.wait()

    grad, hess = small[1], small[2]
    shared = (grad & 3) + jnp.where(hess > 16, 8, 0)
    for at, part in enumerate((grad - shared, hess - 2 * shared, shared)):
        part = jnp.broadcast_to(part.astype(jnp.float32), weights.shape[1:])
        weights[at] = part.astype(weights.dtype)

    wanted_key = lax.broadcasted_iota(jnp.int32, (key_count, row_count), 0).astype(jnp.int8)
    wanted_low = lax.broadcasted_iota(jnp.int32, (LOW, row_count), 0).astype(jnp.int8)
    zero = jnp.zeros((), weights.dtype)
    one = jnp.ones((), weights.dtype)
    first_half = lax.broadcasted_iota(jnp.int32, (3 * key_count, LANES), 1) < LOW
    upper = lax.broadcasted_iota(jnp.int32, (SUBLANES, LANES), 0) < HIGH
    me = place_of(lax.axis_index("rows"), bits)

    def one_hots(feature):
        key = jnp.broadcast_to(row_key[pl.ds(feature, 1), :], (key_count, row_count))
        low = jnp.broadcast_to(low_key[pl.ds(feature, 1), :], (LOW, row_count))
        here = key.astype(jnp.int8) == wanted_key
        left = [
            jnp.where(here, jnp.concatenate([weights[at]] * (key_count // PACKED), axis=0), zero)
            for at in range(3)
        ]
        right = jnp.where(low.astype(jnp.int8) == wanted_low, one, zero)
        return left, right

    for group in range(groups):
        bin_copies[group].wait()
        here = bins[rows_of(group), :]
        row_key[rows_of(group), :] = small[0] * HIGH + (here >> bit_count(LOW))
        low_key[rows_of(group), :] = here & (LOW - 1)
        for pair in range(PAIRS):
            left_a, right_a = one_hots(group * SUBLANES + pair)
            left_b, right_b = one_hots(group * SUBLANES + pair + PAIRS)
            both = lax.dot_general(
                jnp.concatenate(left_a + left_b, axis=0),
                jnp.concatenate([right_a, right_b], axis=0),
                (((1,), (1,)), ((), ())),
                preferred_element_type=jnp.float32,
            )
            own = jnp.where(first_half, both[: 3 * key_count], both[3 * key_count :])
            shared_sum = own[2 * key_count :]
            grad_sum = own[:key_count] + shared_sum
            hess_sum = own[key_count : 2 * key_count] + 2.0 * shared_sum
            for first in range(0, node_count, 2):
                two = slice(first * HIGH, first * HIGH + SUBLANES)
                grads, hesses = grad_sum[two], hess_sum[two]
                tiles = (
                    jnp.where(upper, grads, pltpu.roll(hesses, HIGH, axis=0)),
                    jnp.where(upper, pltpu.roll(grads, HIGH, axis=0), hesses),
                )
                for node, tile in zip((first, first + 1), tiles):
                    table_ref[place_of(node, bits) ^ me, group * PAIRS + pair] = tile


def histograms(bin_index, node_ids, gradients, hessians, node_count):
    feature_count, row_count = bin_index.shape
    return pl.pallas_call(
        histogram_kernel,
        out_shape=jax.ShapeDtypeStruct(
            (node_count, feature_count // 2, NODE_ROWS, LANES), jnp.float32
        ),
        in_specs=[pl.BlockSpec(memory_space=pltpu.HBM)] * 4,
        out_specs=pl.BlockSpec(memory_space=pltpu.VMEM),
        scratch_shapes=[
            pltpu.VMEM((feature_count, row_count), jnp.int32),
            pltpu.VMEM((3, 1, row_count), jnp.int32),
            pltpu.VMEM((feature_count, row_count), jnp.int32),
            pltpu.VMEM((feature_count, row_count), jnp.int32),
            pltpu.VMEM((3, PACKED, row_count), jnp.float8_e4m3fn),
            pltpu.SemaphoreType.DMA((3 + feature_count // SUBLANES,)),
        ],
        compiler_params=pltpu.CompilerParams(vmem_limit_bytes=16 << 20),
        name="histograms",
    )(
        *(
            pltpu.with_memory_space_constraint(array, pltpu.HBM)
            for array in (
                bin_index,
                node_ids.reshape(1, row_count),
                gradients.reshape(1, row_count),
                hessians.reshape(1, row_count),
            )
        )
    )


def summed_over_bins(tiles):
    values = jnp.concatenate(tiles, axis=0)
    parts = []
    for _ in range(3):
        parts.append(values.astype(jnp.bfloat16))
        values = values - parts[-1].astype(jnp.float32)
    source = lax.broadcasted_iota(jnp.int32, (LANES, 2 * LANES), 0)
    column = lax.broadcasted_iota(jnp.int32, (LANES, 2 * LANES), 1)
    counted = jnp.where(source <= column, 1.0, 0.0).astype(jnp.bfloat16)
    sums = lax.dot_general(
        jnp.concatenate(parts, axis=0),
        counted,
        (((1,), (0,)), ((), ())),
        preferred_element_type=jnp.float32,
    )
    count = len(tiles) * tiles[0].shape[0]
    sums = sums[:count] + sums[count : 2 * count] + sums[2 * count :]
    height = tiles[0].shape[0]
    return [
        (sums[at : at + height, :LANES], sums[at : at + height, LANES:])
        for at in range(0, count, height)
    ]


def gains_kernel(own_count, *refs):
    parts, (gains_ref, best_ref, table) = refs[:-3], refs[-3:]
    best = gains_of(parts[:own_count], gains_ref, table)
    if parts[own_count:]:
        best = jnp.maximum(best, gains_of(parts[own_count:], None, table))
    best_ref[...] = best


def gains_of(parts, gains_ref, table):
    pair_count = parts[0].shape[1]
    whole_table = sum(jnp.sum(part[...], axis=0) for part in parts)
    table[...] = whole_table.reshape(pair_count * NODE_ROWS, LANES)
    lane = lax.broadcasted_iota(jnp.int32, (pair_count, LANES), 1)
    tiles = []
    for value in range(2):
        rows = [
            table[pl.ds(value * HIGH + high, pair_count, stride=NODE_ROWS), :]
            for high in range(HIGH)
        ]
        turned = [pltpu.roll(row, LOW, axis=1) for row in rows]
        for at in range(0, HIGH, 2):
            tiles.append(jnp.where(lane < LOW, rows[at], turned[at + 1]))
        for at in range(0, HIGH, 2):
            tiles.append(jnp.where(lane < LOW, turned[at], rows[at + 1]))
    sums = summed_over_bins(tiles)
    best = None
    for half in range(2):
        (grad_0, total_grad_0), (grad_1, total_grad_1) = sums[2 * half : 2 * half + 2]
        (hess_0, total_hess_0), (hess_1, total_hess_1) = sums[4 + 2 * half : 6 + 2 * half]
        total_grad, total_hess = total_grad_0 + total_grad_1, total_hess_0 + total_hess_1
        whole = total_grad * total_grad / (total_hess + shrinkage)
        lefts = ((grad_0, hess_0), (total_grad_0 + grad_1, total_hess_0 + hess_1))
        for at, (left_grad, left_hess) in enumerate(lefts):
            right_grad = total_grad - left_grad
            right_hess = total_hess - left_hess
            gains = 0.5 * (
                left_grad * left_grad / (left_hess + shrinkage)
                + right_grad * right_grad / (right_hess + shrinkage)
                - whole
            )
            if gains_ref is not None:
                for group in range(pair_count // PAIRS):
                    gains_ref[
                        0,
                        pl.ds(group * SUBLANES + half * PAIRS, PAIRS),
                        pl.ds(at * LANES, LANES),
                    ] = gains[group * PAIRS : (group + 1) * PAIRS]
            best = gains if best is None else jnp.maximum(best, gains)
    return best


def split_gains_of(own, others):
    parts = [*own, *others]
    pair_count = parts[0].shape[1]
    return pl.pallas_call(
        functools.partial(gains_kernel, len(own)),
        out_shape=(
            jax.ShapeDtypeStruct((1, 2 * pair_count, BINS), jnp.float32),
            jax.ShapeDtypeStruct((pair_count, LANES), jnp.float32),
        ),
        in_specs=[pl.BlockSpec(memory_space=pltpu.VMEM)] * len(parts),
        out_specs=[pl.BlockSpec(memory_space=pltpu.VMEM)] * 2,
        scratch_shapes=[pltpu.VMEM((pair_count * NODE_ROWS, LANES), jnp.float32)],
        compiler_params=pltpu.CompilerParams(vmem_limit_bytes=8 << 20),
        name="gains",
    )(*parts)


def written_kernel(gains_ref, gains_out):
    gains_out[...] = gains_ref[...]


def written(gains):
    return pl.pallas_call(
        written_kernel,
        out_shape=jax.ShapeDtypeStruct(gains.shape, jnp.float32),
        in_specs=[pl.BlockSpec(memory_space=pltpu.VMEM)],
        out_specs=pl.BlockSpec(memory_space=pltpu.VMEM),
        compiler_params=pltpu.CompilerParams(vmem_limit_bytes=2 << 20),
        cost_estimate=pl.CostEstimate(flops=1 << 20, bytes_accessed=1 << 20, transcendentals=0),
        name="written",
    )(gains)


def swap(array, feat_mask, rows_mask):
    feats, nodes = lax.axis_size("feat"), lax.axis_size("rows")
    pairs = [
        (feat * nodes + node, (feat ^ feat_mask) * nodes + (node ^ rows_mask))
        for feat in range(feats)
        for node in range(nodes)
    ]
    return lax.ppermute(array, ("feat", "rows"), pairs)


def halved(table, phases):
    for phase in phases:
        radix = 1 << len(phase)
        parts = table.reshape(radix, table.shape[0] // radix, *table.shape[1:])
        table = parts[0]
        for part in range(1, radix):
            mask = sum(((part >> (len(phase) - 1 - at)) & 1) << bit for at, bit in enumerate(phase))
            table = table + swap(parts[part], 0, mask)
    return table


def per_device(bin_index, node_ids, gradients, hessians):
    node_count = lax.axis_size("rows")
    table = histograms(bin_index, node_ids, gradients, hessians, node_count)
    phases = phases_of(bit_count(node_count))
    *phases, (last,) = phases
    table = halved(table, phases)
    kept, sent = table[:1], table[1:]
    rows_mask = 1 << last
    own = [kept, swap(sent, 0, rows_mask)]
    others, masks = [], [1 << bit for bit in range(bit_count(lax.axis_size("feat")))]
    if len(masks) > 1:
        pair_mask = masks[0] | masks[1]
        others = [swap(kept, pair_mask, 0), swap(sent, pair_mask, rows_mask)]
        masks = [mask | 1 for mask in masks[2:]] + masks[:1]
    split_gains, best = split_gains_of(own, others)
    other = best
    for mask in masks:
        best = jnp.maximum(best, other)
        other = swap(best, mask, 0)
    best = jnp.max(jnp.maximum(best, other), keepdims=True).reshape(1)
    return written(split_gains), best


def solution(mesh):
    in_specs = (P("feat", "rows"), P("rows"), P("rows"), P("rows"))
    out_specs = (P("rows", "feat", None), P("rows"))
    return jax.shard_map(
        per_device, mesh=mesh, in_specs=in_specs, out_specs=out_specs, check_vma=False
    )
```

```python
import functools

import jax
import jax.numpy as jnp
from jax import lax
from jax.experimental import pallas as pl
from jax.experimental.pallas import tpu as pltpu
from jax.sharding import PartitionSpec as P


BINS = 256
LANES = 128
SUBLANES = 8
PACKED = 32
HIGH = 4
LOW = BINS // HIGH
NODE_ROWS = 2 * HIGH
PAIRS = SUBLANES // 2

shrinkage = 1.0


def bit_count(length):
    return length.bit_length() - 1


def phases_of(bits):
    return [[1, 0]] + [[bit] for bit in range(2, bits)]


def place_of(number, bits):
    order = [bit for phase in phases_of(bits) for bit in phase]
    return sum(((number >> bit) & 1) << (bits - 1 - at) for at, bit in enumerate(order))


def histogram_kernel(
    bin_hbm, node_hbm, grad_hbm, hess_hbm, table_ref, bins, small, row_key, low_key, weights, sems
):
    feature_count, row_count = bins.shape
    node_count = table_ref.shape[0]
    bits = bit_count(node_count)
    key_count = node_count * HIGH
    groups = feature_count // SUBLANES

    def rows_of(group):
        return pl.ds(group * SUBLANES, SUBLANES)

    small_copies = [
        pltpu.make_async_copy(source, small.at[at], sems.at[at])
        for at, source in enumerate((node_hbm, grad_hbm, hess_hbm))
    ]
    bin_copies = [
        pltpu.make_async_copy(bin_hbm.at[rows_of(group)], bins.at[rows_of(group)], sems.at[3 + group])
        for group in range(groups)
    ]
    for copy in small_copies + bin_copies:
        copy.start()
    for copy in small_copies:
        copy.wait()

    grad, hess = small[1], small[2]
    shared = (grad & 3) + jnp.where(hess > 16, 8, 0)
    for at, part in enumerate((grad - shared, hess - 2 * shared, shared)):
        part = jnp.broadcast_to(part.astype(jnp.float32), weights.shape[1:])
        weights[at] = part.astype(weights.dtype)

    wanted_key = lax.broadcasted_iota(jnp.int32, (key_count, row_count), 0).astype(jnp.int8)
    wanted_low = lax.broadcasted_iota(jnp.int32, (LOW, row_count), 0).astype(jnp.int8)
    zero = jnp.zeros((), weights.dtype)
    one = jnp.ones((), weights.dtype)
    first_half = lax.broadcasted_iota(jnp.int32, (3 * key_count, LANES), 1) < LOW
    upper = lax.broadcasted_iota(jnp.int32, (SUBLANES, LANES), 0) < HIGH
    me = place_of(lax.axis_index("rows"), bits)

    def one_hots(feature):
        key = jnp.broadcast_to(row_key[pl.ds(feature, 1), :], (key_count, row_count))
        low = jnp.broadcast_to(low_key[pl.ds(feature, 1), :], (LOW, row_count))
        here = key.astype(jnp.int8) == wanted_key
        left = [
            jnp.where(here, jnp.concatenate([weights[at]] * (key_count // PACKED), axis=0), zero)
            for at in range(3)
        ]
        right = jnp.where(low.astype(jnp.int8) == wanted_low, one, zero)
        return left, right

    for group in range(groups):
        bin_copies[group].wait()
        here = bins[rows_of(group), :]
        row_key[rows_of(group), :] = small[0] * HIGH + (here >> bit_count(LOW))
        low_key[rows_of(group), :] = here & (LOW - 1)
        for pair in range(PAIRS):
            left_a, right_a = one_hots(group * SUBLANES + pair)
            left_b, right_b = one_hots(group * SUBLANES + pair + PAIRS)
            both = lax.dot_general(
                jnp.concatenate(left_a + left_b, axis=0),
                jnp.concatenate([right_a, right_b], axis=0),
                (((1,), (1,)), ((), ())),
                preferred_element_type=jnp.float32,
            )
            own = jnp.where(first_half, both[: 3 * key_count], both[3 * key_count :])
            shared_sum = own[2 * key_count :]
            grad_sum = own[:key_count] + shared_sum
            hess_sum = own[key_count : 2 * key_count] + 2.0 * shared_sum
            for first in range(0, node_count, 2):
                two = slice(first * HIGH, first * HIGH + SUBLANES)
                grads, hesses = grad_sum[two], hess_sum[two]
                tiles = (
                    jnp.where(upper, grads, pltpu.roll(hesses, HIGH, axis=0)),
                    jnp.where(upper, pltpu.roll(grads, HIGH, axis=0), hesses),
                )
                for node, tile in zip((first, first + 1), tiles):
                    table_ref[place_of(node, bits) ^ me, group * PAIRS + pair] = tile


def histograms(bin_index, node_ids, gradients, hessians, node_count):
    feature_count, row_count = bin_index.shape
    return pl.pallas_call(
        histogram_kernel,
        out_shape=jax.ShapeDtypeStruct(
            (node_count, feature_count // 2, NODE_ROWS, LANES), jnp.float32
        ),
        in_specs=[pl.BlockSpec(memory_space=pltpu.HBM)] * 4,
        out_specs=pl.BlockSpec(memory_space=pltpu.VMEM),
        scratch_shapes=[
            pltpu.VMEM((feature_count, row_count), jnp.int32),
            pltpu.VMEM((3, 1, row_count), jnp.int32),
            pltpu.VMEM((feature_count, row_count), jnp.int32),
            pltpu.VMEM((feature_count, row_count), jnp.int32),
            pltpu.VMEM((3, PACKED, row_count), jnp.float8_e4m3fn),
            pltpu.SemaphoreType.DMA((3 + feature_count // SUBLANES,)),
        ],
        compiler_params=pltpu.CompilerParams(vmem_limit_bytes=16 << 20),
        name="histograms",
    )(
        *(
            pltpu.with_memory_space_constraint(array, pltpu.HBM)
            for array in (
                bin_index,
                node_ids.reshape(1, row_count),
                gradients.reshape(1, row_count),
                hessians.reshape(1, row_count),
            )
        )
    )


def summed_over_bins(tiles):
    values = jnp.concatenate(tiles, axis=0)
    parts = []
    for _ in range(3):
        parts.append(values.astype(jnp.bfloat16))
        values = values - parts[-1].astype(jnp.float32)
    source = lax.broadcasted_iota(jnp.int32, (LANES, 2 * LANES), 0)
    column = lax.broadcasted_iota(jnp.int32, (LANES, 2 * LANES), 1)
    counted = jnp.where(source <= column, 1.0, 0.0).astype(jnp.bfloat16)
    sums = lax.dot_general(
        jnp.concatenate(parts, axis=0),
        counted,
        (((1,), (0,)), ((), ())),
        preferred_element_type=jnp.float32,
    )
    count = len(tiles) * tiles[0].shape[0]
    sums = sums[:count] + sums[count : 2 * count] + sums[2 * count :]
    height = tiles[0].shape[0]
    return [
        (sums[at : at + height, :LANES], sums[at : at + height, LANES:])
        for at in range(0, count, height)
    ]


def gains_kernel(own_count, *refs):
    parts, (gains_ref, best_ref, table) = refs[:-3], refs[-3:]
    best = gains_of(parts[:own_count], gains_ref, table)
    if parts[own_count:]:
        best = jnp.maximum(best, gains_of(parts[own_count:], None, table))
    best_ref[...] = jnp.max(best, axis=0, keepdims=True)


def gains_of(parts, gains_ref, table):
    pair_count = parts[0].shape[1]
    whole_table = sum(jnp.sum(part[...], axis=0) for part in parts)
    table[...] = whole_table.reshape(pair_count * NODE_ROWS, LANES)
    lane = lax.broadcasted_iota(jnp.int32, (pair_count, LANES), 1)
    tiles = []
    for value in range(2):
        rows = [
            table[pl.ds(value * HIGH + high, pair_count, stride=NODE_ROWS), :]
            for high in range(HIGH)
        ]
        turned = [pltpu.roll(row, LOW, axis=1) for row in rows]
        for at in range(0, HIGH, 2):
            tiles.append(jnp.where(lane < LOW, rows[at], turned[at + 1]))
        for at in range(0, HIGH, 2):
            tiles.append(jnp.where(lane < LOW, turned[at], rows[at + 1]))
    sums = summed_over_bins(tiles)
    best = None
    for half in range(2):
        (grad_0, total_grad_0), (grad_1, total_grad_1) = sums[2 * half : 2 * half + 2]
        (hess_0, total_hess_0), (hess_1, total_hess_1) = sums[4 + 2 * half : 6 + 2 * half]
        total_grad, total_hess = total_grad_0 + total_grad_1, total_hess_0 + total_hess_1
        whole = total_grad * total_grad / (total_hess + shrinkage)
        lefts = ((grad_0, hess_0), (total_grad_0 + grad_1, total_hess_0 + hess_1))
        for at, (left_grad, left_hess) in enumerate(lefts):
            right_grad = total_grad - left_grad
            right_hess = total_hess - left_hess
            gains = 0.5 * (
                left_grad * left_grad / (left_hess + shrinkage)
                + right_grad * right_grad / (right_hess + shrinkage)
                - whole
            )
            if gains_ref is not None:
                for group in range(pair_count // PAIRS):
                    gains_ref[
                        0,
                        pl.ds(group * SUBLANES + half * PAIRS, PAIRS),
                        pl.ds(at * LANES, LANES),
                    ] = gains[group * PAIRS : (group + 1) * PAIRS]
            best = gains if best is None else jnp.maximum(best, gains)
    return best


def split_gains_of(own, others):
    parts = [*own, *others]
    pair_count = parts[0].shape[1]
    return pl.pallas_call(
        functools.partial(gains_kernel, len(own)),
        out_shape=(
            jax.ShapeDtypeStruct((1, 2 * pair_count, BINS), jnp.float32),
            jax.ShapeDtypeStruct((1, LANES), jnp.float32),
        ),
        in_specs=[pl.BlockSpec(memory_space=pltpu.VMEM)] * len(parts),
        out_specs=[pl.BlockSpec(memory_space=pltpu.VMEM)] * 2,
        scratch_shapes=[pltpu.VMEM((pair_count * NODE_ROWS, LANES), jnp.float32)],
        compiler_params=pltpu.CompilerParams(vmem_limit_bytes=8 << 20),
        name="gains",
    )(*parts)


def written_kernel(gains_ref, gains_out):
    gains_out[...] = gains_ref[...]


def written(gains):
    return pl.pallas_call(
        written_kernel,
        out_shape=jax.ShapeDtypeStruct(gains.shape, jnp.float32),
        in_specs=[pl.BlockSpec(memory_space=pltpu.VMEM)],
        out_specs=pl.BlockSpec(memory_space=pltpu.VMEM),
        compiler_params=pltpu.CompilerParams(vmem_limit_bytes=2 << 20),
        cost_estimate=pl.CostEstimate(flops=1 << 20, bytes_accessed=1 << 20, transcendentals=0),
        name="written",
    )(gains)


def swap(array, feat_mask, rows_mask):
    feats, nodes = lax.axis_size("feat"), lax.axis_size("rows")
    pairs = [
        (feat * nodes + node, (feat ^ feat_mask) * nodes + (node ^ rows_mask))
        for feat in range(feats)
        for node in range(nodes)
    ]
    return lax.ppermute(array, ("feat", "rows"), pairs)


def halved(table, phases):
    for phase in phases:
        radix = 1 << len(phase)
        parts = table.reshape(radix, table.shape[0] // radix, *table.shape[1:])
        table = parts[0]
        for part in range(1, radix):
            mask = sum(((part >> (len(phase) - 1 - at)) & 1) << bit for at, bit in enumerate(phase))
            table = table + swap(parts[part], 0, mask)
    return table


def per_device(bin_index, node_ids, gradients, hessians):
    node_count = lax.axis_size("rows")
    table = histograms(bin_index, node_ids, gradients, hessians, node_count)
    phases = phases_of(bit_count(node_count))
    *phases, (last,) = phases
    table = halved(table, phases)
    kept, sent = table[:1], table[1:]
    rows_mask = 1 << last
    own = [kept, swap(sent, 0, rows_mask)]
    others, masks = [], [1 << bit for bit in range(bit_count(lax.axis_size("feat")))]
    if len(masks) > 1:
        pair_mask = masks[0] | masks[1]
        others = [swap(kept, pair_mask, 0), swap(sent, pair_mask, rows_mask)]
        masks = [mask | 1 for mask in masks[2:]] + masks[:1]
    split_gains, best = split_gains_of(own, others)
    other = best
    for mask in masks:
        best = jnp.maximum(best, other)
        other = swap(best, mask, 0)
    best = jnp.max(jnp.maximum(best, other), keepdims=True).reshape(1)
    return written(split_gains), best


def solution(mesh):
    in_specs = (P("feat", "rows"), P("rows"), P("rows"), P("rows"))
    out_specs = (P("rows", "feat", None), P("rows"))
    return jax.shard_map(
        per_device, mesh=mesh, in_specs=in_specs, out_specs=out_specs, check_vma=False
    )
```
